32 devices in a mesh: wave: 8 (over y, x, core), lev: 4 (over z).
Axes of the slice: x: 2, y: 2, z: 4, core: 2. Of those that a mesh axis runs over, the one named last changes fastest.
Arguments:
- spectra: bfloat16 [2, 128, 1280, 1280], P(None, 'lev', 'wave'), may hold values from -6 to 6
- polynomials: bfloat16 [1280, 1280, 32], P('wave'), may hold values from -0.0048828125 to 0.0048828125
- wave_order: int32 [1280], replicated, may hold values from 0 to 1279, as said below
- row_cutoff: int32 [64], replicated, may hold values from 320 to 1280
Outputs:
- grid: bfloat16 [64, 128, 5120], P(('wave', 'lev'))
The draws below stay inside these ranges and needn't reach their ends.
Inputs may be any that keep to these rules, and one draw needn't show every extreme that they name: `wave_order`: a permutation of the wavenumbers 0 to 1279; slots 2 s and 2 s + 1 hold wavenumbers that add up to 1279.
All inputs are finite; a program needn't handle non-finite values.
Results may differ from the reference program's by a relative error of at most 0.0055.
Values may be sent and summed in bfloat16 or wider, within the bound.
No kernel may reach another device: no remote copies, remote signals or barrier semaphores. Data moves between devices by JAX's collectives and lax.ppermute only.
A program may use at most 448 MiB of HBM per device.

```python
import math
import jax
import jax.numpy as jnp
from jax import lax

WAVES = 1280
NLON = 5120
LEVELS = 128
LATS = 64
HALF = 32


def draw_wave_order(key, part):
    lowers = jax.random.permutation(key, WAVES // 2).astype(jnp.int32)
    paired = jnp.stack([lowers, WAVES - 1 - lowers], axis=1)
    return paired.reshape(WAVES).astype(jnp.int32)


def draw_row_cutoff(key, part):
    first_key, second_key = jax.random.split(key)
    values = jax.random.randint(first_key, (LATS,), WAVES // 4, WAVES + 1).astype(jnp.int32)
    shuffled = jax.random.permutation(second_key, LATS).astype(jnp.int32)
    rows = jnp.arange(LATS, dtype=jnp.int32)
    values = jnp.where(rows == shuffled[0], WAVES, values)
    values = jnp.where(rows == shuffled[1], WAVES // 4, values)
    return values.astype(jnp.int32)


def steps_of(rng, dims, cuts, low, high):
    def one(position, parts):
        heights = jax.random.uniform(jax.random.fold_in(jax.random.fold_in(rng, 6), position), (parts,), jnp.float32, low / len(cuts), high / len(cuts))
        return jnp.repeat(jnp.exp(heights), dims[position] // parts).reshape((-1,) + (1,) * (len(dims) - position - 1))

    loudness = one(*cuts[0])
    for cut in cuts[1:]:
        loudness = loudness * one(*cut)
    return loudness


def normal_values(key, dims, spread, most, shards=(), kind=jnp.bfloat16):
    array = jax.random.normal(key, dims, jnp.float32) * spread
    if len(shards) > 0:
        array = steps_of(key, dims, shards, -0.22, 0.18) * array
    return jnp.clip(array, min=-most, max=most).astype(kind)


def setup_inputs(seed: int = 0) -> dict:
    key_list = jax.random.split(jax.random.key(seed), 5)
    return {
        "spectra": normal_values(key_list[0], (2, LEVELS, WAVES, WAVES), 1.0, 6.0, ((1, 4), (2, 8))),
        "polynomials": normal_values(key_list[1], (WAVES, WAVES, HALF), (WAVES * WAVES) ** -0.5, 0.0048828125, ((0, 8),)),
        "wave_order": draw_wave_order(jax.random.fold_in(key_list[4], 71), 0),
        "row_cutoff": draw_row_cutoff(jax.random.fold_in(key_list[4], 71), 0),
    }


def reference(spectra, polynomials, wave_order, row_cutoff):
    degrees = jnp.arange(WAVES, dtype=jnp.int32)
    limits = WAVES - 1 - wave_order
    parity_sign = jnp.where(degrees % 2 == 0, 1.0, -1.0).astype(jnp.float32)
    block_size = 32 if WAVES % 32 == 0 else WAVES

    def legendre_block(block_start):
        coeffs = lax.dynamic_slice_in_dim(spectra, block_start, block_size, 2).astype(jnp.float32)
        basis_rows = lax.dynamic_slice_in_dim(polynomials, block_start, block_size, 0).astype(jnp.float32)
        bounds = lax.dynamic_slice_in_dim(limits, block_start, block_size, 0)
        usable = degrees[None, :] <= bounds[:, None]
        coeffs = jnp.where(usable[None, None], coeffs, jnp.float32(0.0))
        northern = jnp.einsum("rvkj,kji->rvki", coeffs, basis_rows)
        southern = jnp.einsum("rvkj,kji->rvki", coeffs * parity_sign, basis_rows)
        return jnp.concatenate([northern, southern], axis=3).astype(jnp.bfloat16)

    starts = jnp.arange(WAVES // block_size, dtype=jnp.int32) * block_size
    blocks = lax.map(legendre_block, starts)
    fourier = jnp.transpose(blocks, (4, 1, 2, 0, 3)).reshape(LATS, 2, LEVELS, WAVES)

    longitude = jnp.arange(NLON, dtype=jnp.int32)
    residue = (wave_order[:, None] * longitude[None, :]) % NLON
    angles = residue.astype(jnp.float32) * (2.0 * math.pi / NLON)
    weights = jnp.where(wave_order == 0, 1.0, 2.0).astype(jnp.float32)[:, None]
    phases = jnp.stack([weights * jnp.cos(angles), -weights * jnp.sin(angles)]).astype(jnp.bfloat16)
    phases_wide = phases.astype(jnp.float32)

    def grid_row(items):
        rows, limit = items
        retained = wave_order < limit
        values = jnp.where(retained[None, None, :], rows.astype(jnp.float32), jnp.float32(0.0))
        return jnp.einsum("rvk,rkx->vx", values, phases_wide).astype(jnp.bfloat16)

    return lax.map(grid_row, (fourier, row_cutoff))
```

```python
import functools
import math

import jax
import jax.numpy as jnp
from jax import lax
from jax.experimental import pallas as pl
from jax.experimental.pallas import tpu as pltpu
from jax.sharding import PartitionSpec as P

NLON = 5120
FOLD = NLON // 2
LANES = 128
GROUP = 8
MIB = 1024 * 1024


def nt_dot(left, right):
    return lax.dot_general(
        left, right, (((1,), (1,)), ((), ())), preferred_element_type=jnp.float32
    )


def legendre_kernel(
    first_slot, wave_ref, cut_ref, coeff_ref, basis_ref, out_ref, lhs, pick, rows
):
    parts, levels, _, degrees = coeff_ref.shape
    half = basis_ref.shape[1]
    series = parts * levels
    step = pl.program_id(0)
    slot = lax.axis_index("wave") * first_slot[0] + first_slot[1] + step * GROUP

    @pl.when(step == 0)
    def _():
        source = lax.broadcasted_iota(jnp.int32, pick.shape, 0) // GROUP
        target = lax.broadcasted_iota(jnp.int32, pick.shape, 1) % series
        pick[...] = (source == target).astype(jnp.bfloat16)

    degree = lax.broadcasted_iota(jnp.int32, (1, degrees), 1)
    sign = (1 - 2 * (degree & 1)).astype(jnp.float32)
    waves = [wave_ref[slot + g] for g in range(GROUP)]
    for g in range(GROUP):
        usable = (degree <= degrees - 1 - waves[g]).astype(jnp.float32)
        basis = basis_ref[g]
        lhs[pl.ds(g * half, half), :] = basis * usable.astype(jnp.bfloat16)
        lhs[pl.ds((GROUP + g) * half, half), :] = basis * (usable * sign).astype(jnp.bfloat16)
    coeffs = coeff_ref[...].reshape(series * GROUP, degrees)
    product = nt_dot(lhs[...], coeffs)
    column_slot = lax.broadcasted_iota(jnp.int32, (1, series * GROUP), 1) % GROUP
    for part in range(2):
        for g in range(GROUP):
            block = product[(part * GROUP + g) * half : (part * GROUP + g + 1) * half, :]
            own = jnp.where(column_slot == g, block, 0.0).astype(jnp.bfloat16)
            rows[pl.ds((part * GROUP + g) * half, half), :] = jnp.dot(
                own, pick[...], preferred_element_type=jnp.float32
            )
    sublane = lax.broadcasted_iota(jnp.int32, (GROUP, LANES), 0)
    lane = lax.broadcasted_iota(jnp.int32, (GROUP, LANES), 1)
    wave_column = jnp.zeros((GROUP, LANES), jnp.int32)
    for g in range(GROUP):
        wave_column = jnp.where(sublane == g, waves[g], wave_column)
    rows_here = LANES // series
    for target in range(out_ref.shape[0]):
        value = jnp.zeros((GROUP, LANES), jnp.float32)
        for r in range(rows_here):
            row = target * rows_here + r
            part, i = divmod(row, half)
            loaded = rows[pl.ds(part * GROUP * half + i, GROUP, stride=half), :]
            keep = (lane // series == r) & (wave_column < cut_ref[row])
            value = jnp.where(keep, loaded, value)
        out_ref[target] = value.astype(jnp.bfloat16)


def legendre(spectra, basis, wave_order, row_cutoff, offset, count, targets):
    parts, levels, slots, degrees = spectra.shape
    half = basis.shape[1]
    series = parts * levels
    first = jnp.array([slots, offset], jnp.int32)
    skip = offset // GROUP
    return pl.pallas_call(
        legendre_kernel,
        out_shape=jax.ShapeDtypeStruct((targets, count, LANES), jnp.bfloat16),
        grid_spec=pltpu.PrefetchScalarGridSpec(
            num_scalar_prefetch=3,
            grid=(count // GROUP,),
            in_specs=[
                pl.BlockSpec((parts, levels, GROUP, degrees), lambda g, *_: (0, 0, g + skip, 0)),
                pl.BlockSpec((GROUP, half, degrees), lambda g, *_: (g + skip, 0, 0)),
            ],
            out_specs=pl.BlockSpec((targets, GROUP, LANES), lambda g, *_: (0, g, 0)),
            scratch_shapes=[
                pltpu.VMEM((2 * GROUP * half, degrees), jnp.bfloat16),
                pltpu.VMEM((series * GROUP, LANES), jnp.bfloat16),
                pltpu.VMEM((2 * GROUP * half, LANES), jnp.float32),
            ],
        ),
        compiler_params=pltpu.CompilerParams(vmem_limit_bytes=32 * MIB),
        cost_estimate=pl.CostEstimate(
            flops=4 * count * half * degrees * series * GROUP,
            bytes_accessed=2 * count * degrees * (series + half),
            transcendentals=0,
        ),
        name="legendre",
    )(first, wave_order, row_cutoff, spectra, basis)


def cos_sin(steps):
    turns = jnp.floor(steps * (1.0 / NLON))
    residue = steps - turns * NLON
    quadrant = jnp.floor(residue * (4.0 / NLON) + 0.5)
    angle = (residue - quadrant * (NLON // 4)) * (2.0 * math.pi / NLON)
    square = angle * angle
    cosine = 1.0 + square * (
        -0.5 + square * (1.0 / 24 + square * (-1.0 / 720 + square * (1.0 / 40320)))
    )
    sine = angle * (
        1.0
        + square * (-1.0 / 6 + square * (1.0 / 120 + square * (-1.0 / 5040 + square / 362880.0)))
    )
    turn = quadrant.astype(jnp.int32)
    odd = (turn & 1) == 1
    flip_cos = ((turn + 1) & 2) == 2
    flip_sin = (turn & 2) == 2
    first = jnp.where(odd, sine, cosine)
    second = jnp.where(odd, cosine, sine)
    return jnp.where(flip_cos, -first, first), jnp.where(flip_sin, -second, second)


def table_kernel(layout, wave_ref, out_ref, *, pairs, slots, offset):
    rows = out_ref.shape[2]
    odd_part = pl.program_id(0)
    top = wave_ref.shape[0] - 1
    sublane = lax.broadcasted_iota(jnp.int32, (GROUP, LANES), 0)
    lane = lax.broadcasted_iota(jnp.int32, (GROUP, LANES), 1).astype(jnp.float32)

    for block in range(rows // GROUP):
        column = jnp.zeros((GROUP, LANES), jnp.int32)
        for g in range(GROUP):
            row = pl.program_id(1) * rows + block * GROUP + g
            group = row // pairs
            wave = wave_ref[group * slots + offset + 2 * (row - group * pairs)]
            wave = jnp.where((wave & 1) == odd_part, wave, top - wave)
            column = jnp.where(sublane == g, wave, column)
        wide = column.astype(jnp.float32)
        weight = jnp.where(column == 0, 1.0, 2.0)
        cos_in, sin_in = cos_sin(wide * lane)
        cos_out, sin_out = cos_sin(wide * (lane * LANES))
        cos_in = cos_in * weight
        sin_in = sin_in * weight
        here = pl.ds(block * GROUP, GROUP)
        for o in range(FOLD // LANES):
            c = cos_out[:, o : o + 1]
            s = sin_out[:, o : o + 1]
            span = pl.ds(o * LANES, LANES)
            out_ref[0, 0, here, span] = (c * cos_in - s * sin_in).astype(jnp.bfloat16)
            out_ref[0, 1, here, span] = (-(s * cos_in + c * sin_in)).astype(jnp.bfloat16)


def phase_table(wave_order, groups, slots, offset, count):
    pairs = count // 2
    total = groups * pairs
    rows = 32
    return pl.pallas_call(
        functools.partial(table_kernel, pairs=pairs, slots=slots, offset=offset),
        out_shape=jax.ShapeDtypeStruct((2, 2, total, FOLD), jnp.bfloat16),
        grid_spec=pltpu.PrefetchScalarGridSpec(
            num_scalar_prefetch=2,
            grid=(2, total // rows),
            in_specs=[],
            out_specs=pl.BlockSpec((1, 2, rows, FOLD), lambda p, b, *_: (p, 0, b, 0)),
        ),
        compiler_params=pltpu.CompilerParams(vmem_limit_bytes=16 * MIB),
        cost_estimate=pl.CostEstimate(
            flops=16 * total * FOLD, bytes_accessed=8 * total * FOLD, transcendentals=0
        ),
        name="phases",
    )(jnp.zeros((1,), jnp.int32), wave_order)


def fourier_kernel(wave_ref, got_ref, table_ref, out_ref, left, held, *, levels):
    groups, shards, count, _ = got_ref.shape
    total = groups * count
    pairs = total // 2
    width = table_ref.shape[3]
    steps = FOLD // width
    step = pl.program_id(0)

    @pl.when(step == 0)
    def _():
        row = lax.broadcasted_iota(jnp.int32, (total, total), 0)
        column = lax.broadcasted_iota(jnp.int32, (total, total), 1)
        odd_row = (row >= pairs).astype(jnp.int32)
        chosen = (column // 2 == row - odd_row * pairs) & ((wave_ref[...] & 1) == odd_row)
        sort = chosen.astype(jnp.float32).astype(jnp.bfloat16)
        unit = (
            lax.broadcasted_iota(jnp.int32, (LANES, LANES), 0)
            == lax.broadcasted_iota(jnp.int32, (LANES, LANES), 1)
        ).astype(jnp.float32).astype(jnp.bfloat16)
        for shard in range(shards):
            mine = got_ref[:, shard].reshape(total, LANES)
            sorted_rows = jnp.dot(sort, mine, preferred_element_type=jnp.float32)
            turned = nt_dot(unit, sorted_rows.astype(jnp.bfloat16)).astype(jnp.bfloat16)
            for r in range(LANES // (2 * levels)):
                here = pl.ds(r * shards * levels + shard * levels, levels)
                for part in range(2):
                    at = (2 * r + part) * levels
                    for odd in range(2):
                        left[odd, here, pl.ds(part * pairs, pairs)] = turned[
                            at : at + levels, odd * pairs : (odd + 1) * pairs
                        ]

    @pl.when(step < steps)
    def _():
        sums = [
            jnp.dot(
                left[odd],
                table_ref[odd].reshape(2 * pairs, width),
                preferred_element_type=jnp.float32,
            )
            for odd in range(2)
        ]
        out_ref[...] = (sums[0] + sums[1]).astype(jnp.bfloat16)
        held[step] = (sums[0] - sums[1]).astype(jnp.bfloat16)

    @pl.when(step >= steps)
    def _():
        out_ref[...] = held[step - steps]


def fourier_sum(got, table, wave_order, levels):
    groups, shards, count, _ = got.shape
    total = groups * count
    rows = shards * LANES // 2
    width = 512
    steps = FOLD // width
    return pl.pallas_call(
        functools.partial(fourier_kernel, levels=levels),
        out_shape=jax.ShapeDtypeStruct((rows, NLON), jnp.bfloat16),
        grid_spec=pltpu.PrefetchScalarGridSpec(
            num_scalar_prefetch=0,
            grid=(2 * steps,),
            in_specs=[
                pl.BlockSpec((1, total), lambda x: (0, 0)),
                pl.BlockSpec(got.shape, lambda x: (0, 0, 0, 0)),
                pl.BlockSpec(
                    (2, 2, total // 2, width), lambda x: (0, 0, 0, jnp.minimum(x, steps - 1))
                ),
            ],
            out_specs=pl.BlockSpec((rows, width), lambda x: (0, x)),
            scratch_shapes=[
                pltpu.VMEM((2, rows, total), jnp.bfloat16),
                pltpu.VMEM((steps, rows, width), jnp.bfloat16),
            ],
        ),
        compiler_params=pltpu.CompilerParams(vmem_limit_bytes=48 * MIB),
        cost_estimate=pl.CostEstimate(
            flops=4 * rows * total * FOLD,
            bytes_accessed=4 * total * FOLD + 2 * rows * NLON,
            transcendentals=0,
        ),
        name="fourier",
    )(wave_order.reshape(1, total), got, table)


def local(spectra, polynomials, wave_order, row_cutoff):
    parts, levels, slots, degrees = spectra.shape
    groups = lax.axis_size("wave")
    shards = lax.axis_size("lev")
    targets = groups * shards
    basis = jnp.swapaxes(polynomials, 1, 2)
    sent = legendre(spectra, basis, wave_order, row_cutoff, 0, slots, targets)
    got = lax.all_to_all(sent, ("wave", "lev"), split_axis=0, concat_axis=0, tiled=True)
    table = phase_table(wave_order, groups, slots, 0, slots)
    grid = fourier_sum(got.reshape(groups, shards, slots, LANES), table, wave_order, levels)
    return grid.reshape(LANES // (parts * levels), shards * levels, NLON)


def solution(mesh):
    in_specs = (P(None, "lev", "wave", None), P("wave", None, None), P(), P())
    out_specs = P(("wave", "lev"), None, None)
    return jax.shard_map(local, mesh=mesh, in_specs=in_specs, out_specs=out_specs, check_vma=False)
```

```python
import functools
import math

import jax
import jax.numpy as jnp
from jax import lax
from jax.experimental import pallas as pl
from jax.experimental.pallas import tpu as pltpu
from jax.sharding import PartitionSpec as P

NLON = 5120
FOLD = NLON // 2
LANES = 128
GROUP = 8
WIDTH = 256
VMEM_LIMIT = 60 * 1024 * 1024
DEPTH = 4


def nt_dot(left, right):
    return lax.dot_general(
        left, right, (((1,), (1,)), ((), ())), preferred_element_type=jnp.float32
    )


def one_hot(chosen):
    return chosen.astype(jnp.float32).astype(jnp.bfloat16)


def run_ahead(fetch, step, steps):
    @pl.when(step == 0)
    def _():
        for n in range(min(DEPTH - 1, steps)):
            for copy in fetch(n, n):
                copy.start()

    @pl.when(step + DEPTH - 1 < steps)
    def _():
        for copy in fetch(step + DEPTH - 1, lax.rem(step + DEPTH - 1, DEPTH)):
            copy.start()

    def wait():
        for copy in fetch(step, lax.rem(step, DEPTH)):
            copy.wait()

    return wait


def legendre_kernel(
    wave_ref,
    cut_ref,
    coeff_ref,
    basis_ref,
    out_ref,
    coeff_buffer,
    basis_buffer,
    low,
    high,
    sums,
    sort,
    limits,
    wide,
    tall,
    arrived,
    *,
    offset,
):
    parts, levels, slots, degrees = coeff_ref.shape
    half = basis_ref.shape[1]
    targets, count, _ = out_ref.shape
    batch = sums.shape[0]
    steps = count // GROUP
    pairs = GROUP // 2
    series = parts * levels
    columns = series * GROUP
    cut = low.shape[1]
    step = pl.program_id(0)
    slot = lax.axis_index("wave") * slots + offset + step * GROUP

    def fetch(at, buffer):
        here = pl.ds(pl.multiple_of(offset + at * GROUP, GROUP), GROUP)
        return [
            pltpu.make_async_copy(
                coeff_ref.at[:, :, here, :], coeff_buffer.at[buffer], arrived.at[0, buffer]
            ),
            pltpu.make_async_copy(
                basis_ref.at[here], basis_buffer.at[buffer], arrived.at[1, buffer]
            ),
        ]

    wait = run_ahead(fetch, step, steps)
    buffer = lax.rem(step, DEPTH)

    @pl.when(step == 0)
    def _():
        source = lax.broadcasted_iota(jnp.int32, (columns, columns), 0)
        target = lax.broadcasted_iota(jnp.int32, (columns, columns), 1)
        sort[...] = one_hot(
            (source // GROUP == target % series) & (source % GROUP == target // series)
        )
        for row in range(2 * half):
            limits[pl.ds(row, 1), :] = jnp.full((1, LANES), cut_ref[row], jnp.int32)

    wait()
    degree = lax.broadcasted_iota(jnp.int32, (1, degrees), 1)
    sign = (1 - 2 * (degree & 1)).astype(jnp.float32)
    waves = [wave_ref[slot + g] for g in range(GROUP)]
    longer = [(waves[2 * q] > waves[2 * q + 1]).astype(jnp.int32) for q in range(pairs)]

    def masked(wave, part, begin, end):
        usable = (degree[:, begin:end] <= degrees - 1 - wave).astype(jnp.float32)
        if part == 1:
            usable = usable * sign[:, begin:end]
        return usable.astype(jnp.bfloat16)

    for part in range(2):
        for g in range(GROUP):
            low[pl.ds((part * GROUP + g) * half, half), :] = basis_buffer[
                buffer, g, :, :cut
            ] * masked(waves[g], part, 0, cut)
        for q in range(pairs):
            wave = jnp.minimum(waves[2 * q], waves[2 * q + 1])
            high[pl.ds((part * pairs + q) * half, half), :] = basis_buffer[
                buffer, 2 * q + longer[q], :, cut:
            ] * masked(wave, part, cut, degrees)
    first = nt_dot(low[...], coeff_buffer[buffer, :, :, :, :cut].reshape(columns, cut))
    second = nt_dot(high[...], coeff_buffer[buffer, :, :, :, cut:].reshape(columns, degrees - cut))
    column_slot = lax.broadcasted_iota(jnp.int32, (1, columns), 1) % GROUP
    column_wave = jnp.zeros((1, columns), jnp.int32)
    column_swap = jnp.zeros((1, columns), jnp.int32)
    for g in range(GROUP):
        column_wave = jnp.where(column_slot == g, waves[g], column_wave)
        column_swap = jnp.where(column_slot == g, waves[g // 2 * 2] & 1, column_swap)
    swapped = [(column_swap == 1) & (column_slot % 2 == n) for n in range(2)]
    for part in range(2):
        total = jnp.zeros((half, columns), jnp.float32)
        for q in range(pairs):
            at = (part * pairs + q) * half
            total = jnp.where(column_slot == 2 * q + longer[q], second[at : at + half, :], total)
        for g in range(GROUP):
            at = (part * GROUP + g) * half
            total = total + jnp.where(column_slot == g, first[at : at + half, :], 0.0)
        for tile in range(columns // LANES):
            span = slice(tile * LANES, (tile + 1) * LANES)
            keep = column_wave[:, span] < limits[pl.ds(part * half, half), :]
            kept = jnp.where(keep, total[:, span], 0.0)
            even_first = jnp.where(
                swapped[0][:, span],
                pltpu.roll(kept, LANES - 1, 1),
                jnp.where(swapped[1][:, span], pltpu.roll(kept, 1, 1), kept),
            )
            sums[lax.rem(step, batch), pl.ds(part * half, half), span] = even_first.astype(
                jnp.bfloat16
            )

    @pl.when(lax.rem(step, batch) == batch - 1)
    def _():
        in_order = jnp.dot(
            sums[...].reshape(batch * 2 * half, columns),
            sort[...],
            preferred_element_type=jnp.float32,
        )
        for tile in range(columns // LANES):
            wide[tile] = in_order[:, tile * LANES : (tile + 1) * LANES]
        lane = lax.broadcasted_iota(jnp.int32, (targets, LANES), 1)
        for b in range(batch):
            first_pair = (step - (batch - 1) + b) * pairs
            for q in range(pairs):
                even = wide[q, pl.ds(b * 2 * half, targets, stride=2), :]
                odd = wide[q, pl.ds(b * 2 * half + 1, targets, stride=2), :]
                tall[pl.ds(first_pair + q, targets, stride=count), :] = jnp.where(
                    lane < series, even, pltpu.roll(odd, series, 1)
                )
                tall[pl.ds(count // 2 + first_pair + q, targets, stride=count), :] = jnp.where(
                    lane < series, pltpu.roll(even, series, 1), odd
                )

    @pl.when(step == steps - 1)
    def _():
        out_ref[...] = tall[...].reshape(out_ref.shape).astype(jnp.bfloat16)


def legendre(spectra, basis, wave_order, row_cutoff, offset, count, targets):
    parts, levels, slots, degrees = spectra.shape
    half = basis.shape[1]
    columns = parts * levels * GROUP
    cut = -(-degrees // 2 // 256) * 256
    steps = count // GROUP
    batch = max(n for n in range(1, 6) if steps % n == 0)
    anywhere = pl.BlockSpec(memory_space=pl.ANY)
    return pl.pallas_call(
        functools.partial(legendre_kernel, offset=offset),
        out_shape=jax.ShapeDtypeStruct((targets, count, LANES), jnp.bfloat16),
        grid_spec=pltpu.PrefetchScalarGridSpec(
            num_scalar_prefetch=2,
            grid=(steps,),
            in_specs=[anywhere, anywhere],
            out_specs=pl.BlockSpec((targets, count, LANES), lambda g, *_: (0, 0, 0)),
            scratch_shapes=[
                pltpu.VMEM((DEPTH, parts, levels, GROUP, degrees), jnp.bfloat16),
                pltpu.VMEM((DEPTH, GROUP, half, degrees), jnp.bfloat16),
                pltpu.VMEM((2 * GROUP * half, cut), jnp.bfloat16),
                pltpu.VMEM((GROUP * half, degrees - cut), jnp.bfloat16),
                pltpu.VMEM((batch, 2 * half, columns), jnp.bfloat16),
                pltpu.VMEM((columns, columns), jnp.bfloat16),
                pltpu.VMEM((2 * half, LANES), jnp.int32),
                pltpu.VMEM((columns // LANES, batch * 2 * half, LANES), jnp.float32),
                pltpu.VMEM((targets * count, LANES), jnp.float32),
                pltpu.SemaphoreType.DMA((2, DEPTH)),
            ],
        ),
        compiler_params=pltpu.CompilerParams(vmem_limit_bytes=VMEM_LIMIT),
        cost_estimate=pl.CostEstimate(
            flops=4 * count * half * degrees * columns,
            bytes_accessed=2 * count * degrees * (parts * levels + half),
            transcendentals=0,
        ),
        name="legendre",
    )(wave_order, row_cutoff, spectra, basis)


def cos_sin(steps):
    turns = jnp.floor(steps * (1.0 / NLON))
    residue = steps - turns * NLON
    quadrant = jnp.floor(residue * (4.0 / NLON) + 0.5)
    angle = (residue - quadrant * (NLON // 4)) * (2.0 * math.pi / NLON)
    square = angle * angle
    cosine = 1.0 + square * (
        -0.5 + square * (1.0 / 24 + square * (-1.0 / 720 + square * (1.0 / 40320)))
    )
    sine = angle * (
        1.0
        + square * (-1.0 / 6 + square * (1.0 / 120 + square * (-1.0 / 5040 + square / 362880.0)))
    )
    turn = quadrant.astype(jnp.int32)
    odd = (turn & 1) == 1
    flip_cos = ((turn + 1) & 2) == 2
    flip_sin = (turn & 2) == 2
    first = jnp.where(odd, sine, cosine)
    second = jnp.where(odd, cosine, sine)
    return jnp.where(flip_cos, -first, first), jnp.where(flip_sin, -second, second)


def table_kernel(wave_ref, out_ref, *, stride, count):
    blocks, _, _, _, rows, width = out_ref.shape
    odd_part = pl.program_id(0)
    top = wave_ref.shape[0] - 1
    pairs = min(rows, count // 2)
    sublane = lax.broadcasted_iota(jnp.int32, (GROUP, LANES), 0)
    lane = lax.broadcasted_iota(jnp.int32, (pairs, LANES), 1).astype(jnp.float32)

    @pl.loop(0, rows // pairs)
    def _(at):
        start = (pl.program_id(2) * (rows // pairs) + at) * stride + pl.program_id(1) * count
        waves = []
        for block in range(pairs // GROUP):
            column = jnp.zeros((GROUP, LANES), jnp.int32)
            for g in range(GROUP):
                column = jnp.where(sublane == g, wave_ref[start + 2 * (block * GROUP + g)], column)
            waves.append(column)
        column = jnp.concatenate(waves, axis=0)
        column = jnp.where((column & 1) == odd_part, column, top - column)
        wide = column.astype(jnp.float32)
        weight = jnp.where(column == 0, 1.0, 2.0)
        cosine, sine = cos_sin(wide * lane)
        turn_cos, turn_sin = cos_sin(wide * float(LANES))
        cosine = cosine * weight
        sine = sine * -weight
        here = pl.ds(pl.multiple_of(at * pairs, GROUP), pairs)
        for block in range(blocks):
            for o in range(width // LANES):
                if block + o > 0:
                    cosine, sine = (
                        cosine * turn_cos + sine * turn_sin,
                        sine * turn_cos - cosine * turn_sin,
                    )
                span = pl.ds(o * LANES, LANES)
                out_ref[block, 0, 0, 0, here, span] = cosine.astype(jnp.bfloat16)
                out_ref[block, 0, 0, 1, here, span] = sine.astype(jnp.bfloat16)


def phase_table(wave_order, groups, slots, chunks):
    count = slots // chunks
    total = groups * count // 2
    if chunks == 1:
        rows, stride, count = 64, 128, 128
    else:
        rows, stride = total // 2, slots
    shape = (FOLD // WIDTH, 2, chunks, 2, total, WIDTH)
    return pl.pallas_call(
        functools.partial(table_kernel, stride=stride, count=count),
        out_shape=jax.ShapeDtypeStruct(shape, jnp.bfloat16),
        grid_spec=pltpu.PrefetchScalarGridSpec(
            num_scalar_prefetch=1,
            grid=(2, chunks, total // rows),
            in_specs=[],
            out_specs=pl.BlockSpec(
                (FOLD // WIDTH, 1, 1, 2, rows, WIDTH), lambda p, c, b, *_: (0, p, c, 0, b, 0)
            ),
        ),
        compiler_params=pltpu.CompilerParams(vmem_limit_bytes=VMEM_LIMIT),
        cost_estimate=pl.CostEstimate(
            flops=16 * chunks * total * FOLD,
            bytes_accessed=8 * chunks * total * FOLD,
            transcendentals=0,
        ),
        name="phases",
    )(wave_order)


def arrange(got_ref, left, levels, begin):
    groups, shards, _, pairs, _ = got_ref.shape
    total = groups * pairs
    unit = one_hot(
        lax.broadcasted_iota(jnp.int32, (LANES, LANES), 0)
        == lax.broadcasted_iota(jnp.int32, (LANES, LANES), 1)
    )
    for odd in range(2):
        for shard in range(shards):
            block = got_ref[:, shard, odd].reshape(total, LANES)
            turned = nt_dot(unit, block).astype(jnp.bfloat16)
            for r in range(LANES // (2 * levels)):
                here = pl.ds((r * shards + shard) * levels, levels)
                for part in range(2):
                    at = (2 * r + part) * levels
                    left[odd, here, pl.ds(begin + part * total, total)] = turned[
                        at : at + levels, :
                    ]


def arrange_kernel(got_ref, out_ref, *, levels):
    arrange(got_ref, out_ref, levels, 0)


def arranged(got, levels):
    groups, shards, _, pairs, _ = got.shape
    total = groups * pairs
    rows = shards * LANES // 2
    return pl.pallas_call(
        functools.partial(arrange_kernel, levels=levels),
        out_shape=jax.ShapeDtypeStruct((2, rows, 2 * total), jnp.bfloat16),
        compiler_params=pltpu.CompilerParams(vmem_limit_bytes=VMEM_LIMIT),
        cost_estimate=pl.CostEstimate(
            flops=8 * total * rows * LANES, bytes_accessed=16 * total * rows, transcendentals=0
        ),
        name="arrange",
    )(got)


def fourier_kernel(*refs, levels, chunks):
    early_refs = refs[: chunks - 1]
    got_ref, table_ref, out_ref, table, left, held, arrived, done = refs[chunks - 1 :]
    steps, _, _, _, total, width = table_ref.shape
    span = 2 * total
    step = pl.program_id(0)
    slot = lax.rem(step, 2)

    def fetch(at, buffer):
        return [pltpu.make_async_copy(table_ref.at[at], table.at[buffer], arrived.at[buffer])]

    def copies(at, buffer):
        return [
            pltpu.make_async_copy(
                held.at[buffer, side],
                out_ref.at[:, pl.ds(pl.multiple_of(side * FOLD + at * width, width), width)],
                done.at[buffer, side],
            )
            for side in range(2)
        ]

    wait = run_ahead(fetch, step, steps)

    @pl.when(step == 0)
    def _():
        for chunk, early_ref in enumerate(early_refs):
            left[:, :, pl.ds(chunk * span, span)] = early_ref[...]
        arrange(got_ref, left, levels, (chunks - 1) * span)

    @pl.when(step >= 2)
    def _():
        for copy in copies(step - 2, slot):
            copy.wait()

    wait()
    sums = [
        jnp.dot(
            left[odd],
            table[lax.rem(step, DEPTH), odd].reshape(chunks * span, width),
            preferred_element_type=jnp.float32,
        )
        for odd in range(2)
    ]
    held[slot, 0] = (sums[0] + sums[1]).astype(jnp.bfloat16)
    held[slot, 1] = (sums[0] - sums[1]).astype(jnp.bfloat16)
    for copy in copies(step, slot):
        copy.start()

    @pl.when(step == steps - 1)
    def _():
        for copy in copies(step - 1, 1 - slot) + copies(step, slot):
            copy.wait()


def fourier_sum(early, got, table, levels):
    chunks = len(early) + 1
    groups, shards, _, pairs, _ = got.shape
    total = groups * pairs
    rows = shards * LANES // 2
    whole = pl.BlockSpec(memory_space=pltpu.VMEM)
    anywhere = pl.BlockSpec(memory_space=pl.ANY)
    return pl.pallas_call(
        functools.partial(fourier_kernel, levels=levels, chunks=chunks),
        out_shape=jax.ShapeDtypeStruct((rows, NLON), jnp.bfloat16),
        grid_spec=pltpu.PrefetchScalarGridSpec(
            num_scalar_prefetch=0,
            grid=(FOLD // WIDTH,),
            in_specs=[whole] * chunks + [anywhere],
            out_specs=anywhere,
            scratch_shapes=[
                pltpu.VMEM((DEPTH, *table.shape[1:]), jnp.bfloat16),
                pltpu.VMEM((2, rows, 2 * chunks * total), jnp.bfloat16),
                pltpu.VMEM((2, 2, rows, WIDTH), jnp.bfloat16),
                pltpu.SemaphoreType.DMA((DEPTH,)),
                pltpu.SemaphoreType.DMA((2, 2)),
            ],
        ),
        compiler_params=pltpu.CompilerParams(vmem_limit_bytes=VMEM_LIMIT),
        cost_estimate=pl.CostEstimate(
            flops=8 * rows * chunks * total * FOLD,
            bytes_accessed=8 * chunks * total * FOLD + 2 * rows * NLON,
            transcendentals=0,
        ),
        name="fourier",
    )(*early, got, table)


def local(spectra, polynomials, wave_order, row_cutoff):
    parts, levels, slots, degrees = spectra.shape
    groups = lax.axis_size("wave")
    shards = lax.axis_size("lev")
    basis = jnp.swapaxes(polynomials, 1, 2)
    chunks = 2 if slots % (4 * GROUP) == 0 else 1
    count = slots // chunks
    got = []
    for chunk in range(chunks):
        sent = legendre(
            spectra, basis, wave_order, row_cutoff, chunk * count, count, groups * shards
        )
        arrived = lax.all_to_all(sent, ("wave", "lev"), split_axis=0, concat_axis=0, tiled=True)
        got.append(arrived.reshape(groups, shards, 2, count // 2, LANES))
    table = phase_table(wave_order, groups, slots, chunks)
    early = [arranged(one, levels) for one in got[:-1]]
    grid = fourier_sum(early, got[-1], table, levels)
    return grid.reshape(LANES // (parts * levels), shards * levels, NLON)


def solution(mesh):
    in_specs = (P(None, "lev", "wave", None), P("wave", None, None), P(), P())
    out_specs = P(("wave", "lev"), None, None)
    return jax.shard_map(local, mesh=mesh, in_specs=in_specs, out_specs=out_specs, check_vma=False)
```

```python
import functools
import math

import jax
import jax.numpy as jnp
from jax import lax
from jax.experimental import pallas as pl
from jax.experimental.pallas import tpu as pltpu
from jax.sharding import PartitionSpec as P

NLON = 5120
FOLD = NLON // 4
LANES = 128
GROUP = 8
WIDTH = 256
VMEM_LIMIT = 60 * 1024 * 1024
DEPTH = 3
ROOM = 24


def nt_dot(left, right):
    return lax.dot_general(
        left, right, (((1,), (1,)), ((), ())), preferred_element_type=jnp.float32
    )


def one_hot(chosen):
    return chosen.astype(jnp.float32).astype(jnp.bfloat16)


def run_ahead(fetch, step, steps):
    @pl.when(step == 0)
    def _():
        for n in range(min(DEPTH - 1, steps)):
            for copy in fetch(n, n):
                copy.start()

    @pl.when(step + DEPTH - 1 < steps)
    def _():
        for copy in fetch(step + DEPTH - 1, lax.rem(step + DEPTH - 1, DEPTH)):
            copy.start()

    def wait():
        for copy in fetch(step, lax.rem(step, DEPTH)):
            copy.wait()

    return wait


def legendre_kernel(
    wave_ref,
    cut_ref,
    coeff_ref,
    basis_ref,
    out_ref,
    coeff_buffer,
    basis_buffer,
    low,
    high,
    sums,
    sort,
    limits,
    wide,
    tall,
    arrived,
    *,
    offset,
):
    parts, levels, slots, degrees = coeff_ref.shape
    half = basis_ref.shape[1]
    targets, count, _ = out_ref.shape
    batch = sums.shape[0]
    steps = count // (GROUP * batch)
    pairs = GROUP // 2
    series = parts * levels
    columns = series * GROUP
    cut = low.shape[2]
    step = pl.program_id(0)
    slot = lax.axis_index("wave") * slots + offset + step * batch * GROUP

    def fetch(at, buffer):
        copies = []
        for b in range(batch):
            first = pl.multiple_of(offset + (at * batch + b) * GROUP, GROUP)
            here = pl.ds(first, GROUP)
            copies += [
                pltpu.make_async_copy(
                    coeff_ref.at[:, :, here, :],
                    coeff_buffer.at[buffer, b],
                    arrived.at[0, buffer, b],
                ),
                pltpu.make_async_copy(
                    basis_ref.at[here], basis_buffer.at[buffer, b], arrived.at[1, buffer, b]
                ),
            ]
        return copies

    wait = run_ahead(fetch, step, steps)
    buffer = lax.rem(step, DEPTH)

    @pl.when(step == 0)
    def _():
        source = lax.broadcasted_iota(jnp.int32, (columns, columns), 0)
        target = lax.broadcasted_iota(jnp.int32, (columns, columns), 1)
        sort[...] = one_hot(
            (source // GROUP == target % series) & (source % GROUP == target // series)
        )
        for row in range(2 * half):
            limits[pl.ds(row, 1), :] = jnp.full((1, LANES), cut_ref[row], jnp.int32)

    def spread(at):
        in_order = jnp.dot(
            sums[...].reshape(batch * 2 * half, columns),
            sort[...],
            preferred_element_type=jnp.float32,
        )
        for tile in range(columns // LANES):
            wide[tile] = in_order[:, tile * LANES : (tile + 1) * LANES]
        lane = lax.broadcasted_iota(jnp.int32, (targets, LANES), 1)
        for b in range(batch):
            first_pair = (at * batch + b) * pairs
            for q in range(pairs):
                even = wide[q, pl.ds(b * 2 * half, targets, stride=2), :]
                odd = wide[q, pl.ds(b * 2 * half + 1, targets, stride=2), :]
                tall[pl.ds(first_pair + q, targets, stride=count), :] = jnp.where(
                    lane < series, even, pltpu.roll(odd, series, 1)
                )
                tall[pl.ds(count // 2 + first_pair + q, targets, stride=count), :] = jnp.where(
                    lane < series, pltpu.roll(even, series, 1), odd
                )

    wait()
    spread(jnp.maximum(step - 1, 0))
    degree = lax.broadcasted_iota(jnp.int32, (1, degrees), 1)
    sign = (1 - 2 * (degree & 1)).astype(jnp.float32)

    def masked(wave, part, begin, end):
        usable = (degree[:, begin:end] <= degrees - 1 - wave).astype(jnp.float32)
        if part == 1:
            usable = usable * sign[:, begin:end]
        return usable.astype(jnp.bfloat16)

    waves = [[wave_ref[slot + b * GROUP + g] for g in range(GROUP)] for b in range(batch)]
    longer = [
        [(waves[b][2 * q] > waves[b][2 * q + 1]).astype(jnp.int32) for q in range(pairs)]
        for b in range(batch)
    ]
    for b in range(batch):
        for part in range(2):
            for g in range(GROUP):
                low[b, pl.ds((part * GROUP + g) * half, half), :] = basis_buffer[
                    buffer, b, g, :, :cut
                ] * masked(waves[b][g], part, 0, cut)
            for q in range(pairs):
                wave = jnp.minimum(waves[b][2 * q], waves[b][2 * q + 1])
                high[b, pl.ds((part * pairs + q) * half, half), :] = basis_buffer[
                    buffer, b, 2 * q + longer[b][q], :, cut:
                ] * masked(wave, part, cut, degrees)
    column_slot = lax.broadcasted_iota(jnp.int32, (1, columns), 1) % GROUP
    for b in range(batch):
        first = nt_dot(low[b], coeff_buffer[buffer, b, :, :, :, :cut].reshape(columns, cut))
        second = nt_dot(
            high[b], coeff_buffer[buffer, b, :, :, :, cut:].reshape(columns, degrees - cut)
        )
        column_wave = jnp.zeros((1, columns), jnp.int32)
        column_swap = jnp.zeros((1, columns), jnp.int32)
        for g in range(GROUP):
            column_wave = jnp.where(column_slot == g, waves[b][g], column_wave)
            column_swap = jnp.where(column_slot == g, waves[b][g // 2 * 2] & 1, column_swap)
        swapped = [(column_swap == 1) & (column_slot % 2 == n) for n in range(2)]
        for part in range(2):
            total = jnp.zeros((half, columns), jnp.float32)
            for q in range(pairs):
                at = (part * pairs + q) * half
                total = jnp.where(
                    column_slot == 2 * q + longer[b][q], second[at : at + half, :], total
                )
            own = jnp.zeros((half, columns), jnp.float32)
            for g in range(GROUP):
                at = (part * GROUP + g) * half
                own = jnp.where(column_slot == g, first[at : at + half, :], own)
            total = total + own
            for tile in range(columns // LANES):
                span = slice(tile * LANES, (tile + 1) * LANES)
                keep = column_wave[:, span] < limits[pl.ds(part * half, half), :]
                kept = jnp.where(keep, total[:, span], 0.0)
                even_first = jnp.where(
                    swapped[0][:, span],
                    pltpu.roll(kept, LANES - 1, 1),
                    jnp.where(swapped[1][:, span], pltpu.roll(kept, 1, 1), kept),
                )
                sums[b, pl.ds(part * half, half), span] = even_first.astype(jnp.bfloat16)

    @pl.when(step == steps - 1)
    def _():
        spread(step)
        out_ref[...] = tall[...].reshape(out_ref.shape).astype(jnp.bfloat16)


def legendre(spectra, basis, wave_order, row_cutoff, offset, count, targets):
    parts, levels, slots, degrees = spectra.shape
    half = basis.shape[1]
    columns = parts * levels * GROUP
    cut = -(-degrees // 2 // 256) * 256
    batch = 2 if count % (2 * GROUP) == 0 else 1
    steps = count // (batch * GROUP)
    anywhere = pl.BlockSpec(memory_space=pl.ANY)
    return pl.pallas_call(
        functools.partial(legendre_kernel, offset=offset),
        out_shape=jax.ShapeDtypeStruct((targets, count, LANES), jnp.bfloat16),
        grid_spec=pltpu.PrefetchScalarGridSpec(
            num_scalar_prefetch=2,
            grid=(steps,),
            in_specs=[anywhere, anywhere],
            out_specs=pl.BlockSpec((targets, count, LANES), lambda g, *_: (0, 0, 0)),
            scratch_shapes=[
                pltpu.VMEM((DEPTH, batch, parts, levels, GROUP, degrees), jnp.bfloat16),
                pltpu.VMEM((DEPTH, batch, GROUP, half, degrees), jnp.bfloat16),
                pltpu.VMEM((batch, 2 * GROUP * half, cut), jnp.bfloat16),
                pltpu.VMEM((batch, GROUP * half, degrees - cut), jnp.bfloat16),
                pltpu.VMEM((batch, 2 * half, columns), jnp.bfloat16),
                pltpu.VMEM((columns, columns), jnp.bfloat16),
                pltpu.VMEM((2 * half, LANES), jnp.int32),
                pltpu.VMEM((columns // LANES, batch * 2 * half, LANES), jnp.float32),
                pltpu.VMEM((targets * count, LANES), jnp.float32),
                pltpu.SemaphoreType.DMA((2, DEPTH, batch)),
            ],
        ),
        compiler_params=pltpu.CompilerParams(vmem_limit_bytes=VMEM_LIMIT),
        cost_estimate=pl.CostEstimate(
            flops=4 * count * half * degrees * columns,
            bytes_accessed=2 * count * degrees * (parts * levels + half),
            transcendentals=0,
        ),
        name="legendre",
    )(wave_order, row_cutoff, spectra, basis)


def cos_sin(steps):
    turns = jnp.floor(steps * (1.0 / NLON))
    residue = steps - turns * NLON
    quadrant = jnp.floor(residue * (4.0 / NLON) + 0.5)
    angle = (residue - quadrant * (NLON // 4)) * (2.0 * math.pi / NLON)
    square = angle * angle
    cosine = 1.0 + square * (
        -0.5 + square * (1.0 / 24 + square * (-1.0 / 720 + square * (1.0 / 40320)))
    )
    sine = angle * (
        1.0
        + square * (-1.0 / 6 + square * (1.0 / 120 + square * (-1.0 / 5040 + square / 362880.0)))
    )
    turn = quadrant.astype(jnp.int32)
    odd = (turn & 1) == 1
    flip_cos = ((turn + 1) & 2) == 2
    flip_sin = (turn & 2) == 2
    first = jnp.where(odd, sine, cosine)
    second = jnp.where(odd, cosine, sine)
    return jnp.where(flip_cos, -first, first), jnp.where(flip_sin, -second, second)


def table_kernel(wave_ref, out_ref, *, segments):
    odd_part = pl.program_id(0)
    top = wave_ref.shape[0] - 1
    sublane = lax.broadcasted_iota(jnp.int32, (GROUP, LANES), 0)
    begin = 0
    for groups, stride, first, pairs in segments:
        lane = lax.broadcasted_iota(jnp.int32, (pairs, LANES), 1).astype(jnp.float32)

        @pl.loop(0, groups)
        def _(group):
            waves = []
            for block in range(0, pairs, GROUP):
                column = jnp.zeros((GROUP, LANES), jnp.int32)
                for g in range(GROUP):
                    wave = wave_ref[group * stride + first + 2 * (block + g)]
                    column = jnp.where(sublane == g, wave, column)
                waves.append(column)
            column = jnp.concatenate(waves, axis=0)
            column = jnp.where((column & 1) == odd_part, column, top - column)
            wide = column.astype(jnp.float32)
            weight = jnp.where(column == 0, 1.0, 2.0)
            cosine, sine = cos_sin(wide * lane)
            turn_cos, turn_sin = cos_sin(wide * float(LANES))
            cosine = cosine * weight
            sine = sine * -weight
            here = pl.ds(pl.multiple_of(begin + group * pairs, GROUP), pairs)
            for tile in range(FOLD // LANES + 1):
                if tile > 0:
                    cosine, sine = (
                        cosine * turn_cos + sine * turn_sin,
                        sine * turn_cos - cosine * turn_sin,
                    )
                block, at = divmod(tile * LANES, WIDTH)
                out_ref[block, 0, 0, here, pl.ds(at, LANES)] = cosine.astype(jnp.bfloat16)
                out_ref[block, 0, 1, here, pl.ds(at, LANES)] = sine.astype(jnp.bfloat16)

        begin += groups * pairs


def phase_table(wave_order, slots, counts):
    waves = wave_order.shape[0]
    pairs = waves // 2
    if len(counts) == 1:
        segments = ((waves // 64, 64, 0, 32),)
    else:
        segments = tuple(
            (waves // slots, slots, sum(counts[:n]), count // 2) for n, count in enumerate(counts)
        )
    blocks = FOLD // WIDTH + 1
    return pl.pallas_call(
        functools.partial(table_kernel, segments=segments),
        out_shape=jax.ShapeDtypeStruct((blocks, 2, 2, pairs, WIDTH), jnp.bfloat16),
        grid_spec=pltpu.PrefetchScalarGridSpec(
            num_scalar_prefetch=1,
            grid=(2,),
            in_specs=[],
            out_specs=pl.BlockSpec(
                (blocks, 1, 2, pairs, WIDTH), lambda p, *_: (0, p, 0, 0, 0)
            ),
        ),
        compiler_params=pltpu.CompilerParams(vmem_limit_bytes=VMEM_LIMIT),
        cost_estimate=pl.CostEstimate(
            flops=16 * waves * FOLD, bytes_accessed=4 * waves * FOLD, transcendentals=0
        ),
        name="phases",
    )(wave_order)


def arrange(got_ref, left, levels, begin):
    groups, shards, _, pairs, _ = got_ref.shape
    total = groups * pairs
    unit = one_hot(
        lax.broadcasted_iota(jnp.int32, (LANES, LANES), 0)
        == lax.broadcasted_iota(jnp.int32, (LANES, LANES), 1)
    )
    for odd in range(2):
        for shard in range(shards):
            block = got_ref[:, shard, odd].reshape(total, LANES)
            turned = nt_dot(unit, block).astype(jnp.bfloat16)
            for r in range(LANES // (2 * levels)):
                here = pl.ds((r * shards + shard) * levels, levels)
                for part in range(2):
                    at = (2 * r + part) * levels
                    left[odd, part, here, pl.ds(begin, total)] = turned[at : at + levels, :]


def arrange_kernel(got_ref, out_ref, *, levels):
    arrange(got_ref, out_ref.at[0], levels, 0)


def arranged(got, levels):
    groups, shards, _, pairs, _ = got.shape
    total = groups * pairs
    rows = shards * LANES // 2
    return pl.pallas_call(
        functools.partial(arrange_kernel, levels=levels),
        out_shape=jax.ShapeDtypeStruct((ROOM, 2, 2, rows, total), jnp.bfloat16),
        grid=(1,),
        in_specs=[pl.BlockSpec(got.shape, lambda g: (0, 0, 0, 0, 0))],
        out_specs=pl.BlockSpec((1, 2, 2, rows, total), lambda g: (0, 0, 0, 0, 0)),
        compiler_params=pltpu.CompilerParams(vmem_limit_bytes=VMEM_LIMIT),
        cost_estimate=pl.CostEstimate(
            flops=8 * total * rows * LANES, bytes_accessed=16 * total * rows, transcendentals=0
        ),
        name="arrange",
    )(got)


def fourier_kernel(*refs, levels, early):
    early_refs = refs[:early]
    got_ref, table_ref, out_ref = refs[early : early + 3]
    got, table, edge, left, back, result, fetched, arrived, done = refs[early + 3 :]
    blocks = table_ref.shape[0] - 1
    moves = [pltpu.make_async_copy(got_ref, got, fetched.at[0])]
    edge_move = pltpu.make_async_copy(
        table_ref.at[blocks, :, :, :, pl.ds(0, LANES)], edge, fetched.at[1]
    )
    begin = 0
    for n, early_ref in enumerate(early_refs):
        span = early_ref.shape[4]
        target = left.at[:, :, :, pl.ds(begin, span)]
        moves.append(pltpu.make_async_copy(early_ref.at[0], target, fetched.at[n + 2]))
        begin += span
    order = list(range(blocks - 1, -1, -1))
    tables = {
        at: pltpu.make_async_copy(table_ref.at[at], table.at[at], arrived.at[at]) for at in order
    }
    for move in moves:
        move.start()
    for at in order:
        tables[at].start()
    edge_move.start()
    moves[0].wait()
    arrange(got, left, levels, begin)
    for move in moves[1:]:
        move.wait()

    def combine(block):
        sums = [
            [
                jnp.dot(left[odd, part], block[odd, part], preferred_element_type=jnp.float32)
                for part in range(2)
            ]
            for odd in range(2)
        ]
        return [
            (sums[0][part] + sums[1][part], sums[0][part] - sums[1][part]) for part in range(2)
        ]

    mirror = one_hot(
        lax.broadcasted_iota(jnp.int32, (2 * LANES, LANES), 0)
        == LANES - lax.broadcasted_iota(jnp.int32, (2 * LANES, LANES), 1)
    )
    stores = []

    def reverse(first, tile):
        for side in range(2):
            turned = jnp.dot(
                back[side, :, pl.ds(first + tile * LANES, 2 * LANES)],
                mirror,
                preferred_element_type=jnp.float32,
            )
            to = (2 * side + 2) * FOLD - first - (tile + 1) * LANES
            result[:, pl.ds(to, LANES)] = turned.astype(jnp.bfloat16)

    def store(at, n, start):
        span = pl.ds(start, WIDTH)
        copy = pltpu.make_async_copy(result.at[:, span], out_ref.at[:, span], done.at[at, n])
        copy.start()
        stores.append(copy)

    tiles = WIDTH // LANES
    for at in order:
        tables[at].wait()
        (a, c), (b, d) = combine(table.at[at])
        first = at * WIDTH
        result[:, pl.ds(first, WIDTH)] = (a + b).astype(jnp.bfloat16)
        result[:, pl.ds(2 * FOLD + first, WIDTH)] = (c + d).astype(jnp.bfloat16)
        back[0, :, pl.ds(first, WIDTH)] = (c - d).astype(jnp.bfloat16)
        back[1, :, pl.ds(first, WIDTH)] = (a - b).astype(jnp.bfloat16)
        store(at, 0, first)
        store(at, 1, 2 * FOLD + first)
        outermost = at == blocks - 1
        for tile in range(tiles - 1 if outermost else tiles):
            reverse(first, tile)
        if not outermost:
            store(at, 2, 2 * FOLD - first - WIDTH)
            store(at, 3, 4 * FOLD - first - WIDTH)
    edge_move.wait()
    (a, c), (b, d) = combine(edge)
    back[0, :, pl.ds(FOLD, LANES)] = (c - d).astype(jnp.bfloat16)
    back[1, :, pl.ds(FOLD, LANES)] = (a - b).astype(jnp.bfloat16)
    reverse(FOLD - WIDTH, tiles - 1)
    store(blocks - 1, 2, FOLD)
    store(blocks - 1, 3, 3 * FOLD)
    for copy in stores:
        copy.wait()


def fourier_sum(early, got, table, levels):
    shards = got.shape[1]
    rows = shards * LANES // 2
    blocks, _, _, pairs, _ = table.shape
    blocks -= 1
    anywhere = pl.BlockSpec(memory_space=pl.ANY)
    return pl.pallas_call(
        functools.partial(fourier_kernel, levels=levels, early=len(early)),
        out_shape=jax.ShapeDtypeStruct((rows, NLON), jnp.bfloat16),
        in_specs=[anywhere] * (len(early) + 2),
        out_specs=anywhere,
        scratch_shapes=[
            pltpu.VMEM(got.shape, jnp.bfloat16),
            pltpu.VMEM((blocks, *table.shape[1:]), jnp.bfloat16),
            pltpu.VMEM((2, 2, pairs, LANES), jnp.bfloat16),
            pltpu.VMEM((2, 2, rows, pairs), jnp.bfloat16),
            pltpu.VMEM((2, rows, FOLD + LANES), jnp.bfloat16),
            pltpu.VMEM((rows, NLON), jnp.bfloat16),
            pltpu.SemaphoreType.DMA((len(early) + 2,)),
            pltpu.SemaphoreType.DMA((blocks,)),
            pltpu.SemaphoreType.DMA((blocks, 4)),
        ],
        compiler_params=pltpu.CompilerParams(vmem_limit_bytes=52 * 1024 * 1024),
        cost_estimate=pl.CostEstimate(
            flops=8 * rows * pairs * FOLD,
            bytes_accessed=8 * pairs * FOLD + 2 * rows * NLON,
            transcendentals=0,
        ),
        name="fourier",
    )(*early, got, table)


def chunk_counts(slots):
    if slots % (4 * GROUP):
        return (slots,)
    first = slots * 2 // 5 // (2 * GROUP) * (2 * GROUP)
    return (first, slots - first)


def local(spectra, polynomials, wave_order, row_cutoff):
    parts, levels, slots, degrees = spectra.shape
    groups = lax.axis_size("wave")
    shards = lax.axis_size("lev")
    basis = jnp.swapaxes(polynomials, 1, 2)
    counts = chunk_counts(slots)
    got = []
    for chunk, count in enumerate(counts):
        sent = legendre(
            spectra, basis, wave_order, row_cutoff, sum(counts[:chunk]), count, groups * shards
        )
        arrived = lax.all_to_all(sent, ("wave", "lev"), split_axis=0, concat_axis=0, tiled=True)
        got.append(arrived.reshape(groups, shards, 2, count // 2, LANES))
    table = phase_table(wave_order, slots, counts)
    early = [arranged(one, levels) for one in got[:-1]]
    grid = fourier_sum(early, got[-1], table, levels)
    return grid.reshape(LANES // (parts * levels), shards * levels, NLON)


def solution(mesh):
    in_specs = (P(None, "lev", "wave", None), P("wave", None, None), P(), P())
    out_specs = P(("wave", "lev"), None, None)
    return jax.shard_map(local, mesh=mesh, in_specs=in_specs, out_specs=out_specs, check_vma=False)
```

```python
import functools
import math

import jax
import jax.numpy as jnp
from jax import lax
from jax.experimental import pallas as pl
from jax.experimental.pallas import tpu as pltpu
from jax.sharding import PartitionSpec as P

NLON = 5120
FOLD = NLON // 4
LANES = 128
GROUP = 8
WIDTH = 256
VMEM_LIMIT = 60 * 1024 * 1024
DEPTH = 3


def nt_dot(left, right):
    return lax.dot_general(
        left, right, (((1,), (1,)), ((), ())), preferred_element_type=jnp.float32
    )


def one_hot(chosen):
    return chosen.astype(jnp.float32).astype(jnp.bfloat16)


def run_ahead(fetch, step, steps):
    @pl.when(step == 0)
    def _():
        for n in range(min(DEPTH - 1, steps)):
            for copy in fetch(n, n):
                copy.start()

    @pl.when(step + DEPTH - 1 < steps)
    def _():
        for copy in fetch(step + DEPTH - 1, lax.rem(step + DEPTH - 1, DEPTH)):
            copy.start()

    def wait():
        for copy in fetch(step, lax.rem(step, DEPTH)):
            copy.wait()

    return wait


def legendre_kernel(
    wave_ref,
    cut_ref,
    coeff_ref,
    basis_ref,
    *refs,
    offset,
    groups,
    shards,
):
    parts, levels, slots, degrees = coeff_ref.shape
    half = basis_ref.shape[1]
    out_refs = refs[:-10]
    coeff_buffer, basis_buffer, low, high, sums, sort, limits, wide, tall, arrived = refs[-10:]
    count = out_refs[0].shape[1]
    targets = groups * shards
    batch = sums.shape[0]
    steps = count // (GROUP * batch)
    pairs = GROUP // 2
    series = parts * levels
    columns = series * GROUP
    cut = low.shape[2]
    step = pl.program_id(0)
    slot = lax.axis_index("wave") * slots + offset + step * batch * GROUP

    def fetch(at, buffer):
        copies = []
        for b in range(batch):
            first = pl.multiple_of(offset + (at * batch + b) * GROUP, GROUP)
            here = pl.ds(first, GROUP)
            copies += [
                pltpu.make_async_copy(
                    coeff_ref.at[:, :, here, :],
                    coeff_buffer.at[buffer, b],
                    arrived.at[0, buffer, b],
                ),
                pltpu.make_async_copy(
                    basis_ref.at[here], basis_buffer.at[buffer, b], arrived.at[1, buffer, b]
                ),
            ]
        return copies

    wait = run_ahead(fetch, step, steps)
    buffer = lax.rem(step, DEPTH)

    @pl.when(step == 0)
    def _():
        source = lax.broadcasted_iota(jnp.int32, (columns, columns), 0)
        target = lax.broadcasted_iota(jnp.int32, (columns, columns), 1)
        sort[...] = one_hot(
            (source // GROUP == target % series) & (source % GROUP == target // series)
        )
        for row in range(2 * half):
            limits[pl.ds(row, 1), :] = jnp.full((1, LANES), cut_ref[row], jnp.int32)

    def spread(at):
        in_order = jnp.dot(
            sums[...].reshape(batch * 2 * half, columns),
            sort[...],
            preferred_element_type=jnp.float32,
        )
        for tile in range(columns // LANES):
            wide[tile] = in_order[:, tile * LANES : (tile + 1) * LANES]
        lane = lax.broadcasted_iota(jnp.int32, (targets, LANES), 1)
        for b in range(batch):
            first_pair = (at * batch + b) * pairs
            for q in range(pairs):
                even = wide[q, pl.ds(b * 2 * half, targets, stride=2), :]
                odd = wide[q, pl.ds(b * 2 * half + 1, targets, stride=2), :]
                tall[pl.ds(first_pair + q, targets, stride=count), :] = jnp.where(
                    lane < series, even, pltpu.roll(odd, series, 1)
                )
                tall[pl.ds(count // 2 + first_pair + q, targets, stride=count), :] = jnp.where(
                    lane < series, pltpu.roll(even, series, 1), odd
                )

    wait()
    spread(jnp.maximum(step - 1, 0))
    degree = lax.broadcasted_iota(jnp.int32, (1, degrees), 1)
    sign = (1 - 2 * (degree & 1)).astype(jnp.float32)

    def masked(wave, part, begin, end):
        usable = (degree[:, begin:end] <= degrees - 1 - wave).astype(jnp.float32)
        if part == 1:
            usable = usable * sign[:, begin:end]
        return usable.astype(jnp.bfloat16)

    waves = [[wave_ref[slot + b * GROUP + g] for g in range(GROUP)] for b in range(batch)]
    longer = [
        [(waves[b][2 * q] > waves[b][2 * q + 1]).astype(jnp.int32) for q in range(pairs)]
        for b in range(batch)
    ]
    for b in range(batch):
        for part in range(2):
            for g in range(GROUP):
                low[b, pl.ds((part * GROUP + g) * half, half), :] = basis_buffer[
                    buffer, b, g, :, :cut
                ] * masked(waves[b][g], part, 0, cut)
            for q in range(pairs):
                wave = jnp.minimum(waves[b][2 * q], waves[b][2 * q + 1])
                high[b, pl.ds((part * pairs + q) * half, half), :] = basis_buffer[
                    buffer, b, 2 * q + longer[b][q], :, cut:
                ] * masked(wave, part, cut, degrees)
    column_slot = lax.broadcasted_iota(jnp.int32, (1, columns), 1) % GROUP
    for b in range(batch):
        first = nt_dot(low[b], coeff_buffer[buffer, b, :, :, :, :cut].reshape(columns, cut))
        second = nt_dot(
            high[b], coeff_buffer[buffer, b, :, :, :, cut:].reshape(columns, degrees - cut)
        )
        column_wave = jnp.zeros((1, columns), jnp.int32)
        column_swap = jnp.zeros((1, columns), jnp.int32)
        for g in range(GROUP):
            column_wave = jnp.where(column_slot == g, waves[b][g], column_wave)
            column_swap = jnp.where(column_slot == g, waves[b][g // 2 * 2] & 1, column_swap)
        swapped = [(column_swap == 1) & (column_slot % 2 == n) for n in range(2)]
        for part in range(2):
            total = jnp.zeros((half, columns), jnp.float32)
            for q in range(pairs):
                at = (part * pairs + q) * half
                total = jnp.where(
                    column_slot == 2 * q + longer[b][q], second[at : at + half, :], total
                )
            own = jnp.zeros((half, columns), jnp.float32)
            for g in range(GROUP):
                at = (part * GROUP + g) * half
                own = jnp.where(column_slot == g, first[at : at + half, :], own)
            total = total + own
            for tile in range(columns // LANES):
                span = slice(tile * LANES, (tile + 1) * LANES)
                keep = column_wave[:, span] < limits[pl.ds(part * half, half), :]
                kept = jnp.where(keep, total[:, span], 0.0)
                even_first = jnp.where(
                    swapped[0][:, span],
                    pltpu.roll(kept, LANES - 1, 1),
                    jnp.where(swapped[1][:, span], pltpu.roll(kept, 1, 1), kept),
                )
                sums[b, pl.ds(part * half, half), span] = even_first.astype(jnp.bfloat16)

    @pl.when(step == steps - 1)
    def _():
        spread(step)
        if len(out_refs) == 1:
            out_refs[0][...] = tall[...].reshape(out_refs[0].shape).astype(jnp.bfloat16)
            return
        for shift, out_ref in enumerate(out_refs):
            for turn in range(groups):
                target = (lax.axis_index("wave") ^ turn) * shards + (
                    lax.axis_index("lev") ^ shift
                )
                here = pl.ds(pl.multiple_of(target * count, GROUP), count)
                out_ref[turn] = tall[here, :].astype(jnp.bfloat16)


def legendre(spectra, basis, wave_order, row_cutoff, offset, count, groups, shards, relative):
    parts, levels, slots, degrees = spectra.shape
    half = basis.shape[1]
    columns = parts * levels * GROUP
    cut = -(-degrees // 2 // 256) * 256
    batch = 2 if count % (2 * GROUP) == 0 else 1
    steps = count // (batch * GROUP)
    targets = groups * shards
    outs, blocks = (shards, groups) if relative else (1, targets)
    anywhere = pl.BlockSpec(memory_space=pl.ANY)
    return pl.pallas_call(
        functools.partial(legendre_kernel, offset=offset, groups=groups, shards=shards),
        out_shape=[jax.ShapeDtypeStruct((blocks, count, LANES), jnp.bfloat16)] * outs,
        grid_spec=pltpu.PrefetchScalarGridSpec(
            num_scalar_prefetch=2,
            grid=(steps,),
            in_specs=[anywhere, anywhere],
            out_specs=[pl.BlockSpec((blocks, count, LANES), lambda g, *_: (0, 0, 0))] * outs,
            scratch_shapes=[
                pltpu.VMEM((DEPTH, batch, parts, levels, GROUP, degrees), jnp.bfloat16),
                pltpu.VMEM((DEPTH, batch, GROUP, half, degrees), jnp.bfloat16),
                pltpu.VMEM((batch, 2 * GROUP * half, cut), jnp.bfloat16),
                pltpu.VMEM((batch, GROUP * half, degrees - cut), jnp.bfloat16),
                pltpu.VMEM((batch, 2 * half, columns), jnp.bfloat16),
                pltpu.VMEM((columns, columns), jnp.bfloat16),
                pltpu.VMEM((2 * half, LANES), jnp.int32),
                pltpu.VMEM((columns // LANES, batch * 2 * half, LANES), jnp.float32),
                pltpu.VMEM((targets * count, LANES), jnp.float32),
                pltpu.SemaphoreType.DMA((2, DEPTH, batch)),
            ],
        ),
        compiler_params=pltpu.CompilerParams(vmem_limit_bytes=VMEM_LIMIT),
        cost_estimate=pl.CostEstimate(
            flops=4 * count * half * degrees * columns,
            bytes_accessed=2 * count * degrees * (parts * levels + half),
            transcendentals=0,
        ),
        name="legendre",
    )(wave_order, row_cutoff, spectra, basis)


def cos_sin(steps):
    turns = jnp.floor(steps * (1.0 / NLON))
    residue = steps - turns * NLON
    quadrant = jnp.floor(residue * (4.0 / NLON) + 0.5)
    angle = (residue - quadrant * (NLON // 4)) * (2.0 * math.pi / NLON)
    square = angle * angle
    cosine = 1.0 + square * (
        -0.5 + square * (1.0 / 24 + square * (-1.0 / 720 + square * (1.0 / 40320)))
    )
    sine = angle * (
        1.0
        + square * (-1.0 / 6 + square * (1.0 / 120 + square * (-1.0 / 5040 + square / 362880.0)))
    )
    turn = quadrant.astype(jnp.int32)
    odd = (turn & 1) == 1
    flip_cos = ((turn + 1) & 2) == 2
    flip_sin = (turn & 2) == 2
    first = jnp.where(odd, sine, cosine)
    second = jnp.where(odd, cosine, sine)
    return jnp.where(flip_cos, -first, first), jnp.where(flip_sin, -second, second)


def table_kernel(wave_ref, out_ref, *, segments):
    odd_part = pl.program_id(0)
    top = wave_ref.shape[0] - 1
    sublane = lax.broadcasted_iota(jnp.int32, (GROUP, LANES), 0)
    begin = 0
    for groups, stride, first, pairs, relative in segments:
        mask = lax.axis_index("wave") if relative else 0
        lane = lax.broadcasted_iota(jnp.int32, (pairs, LANES), 1).astype(jnp.float32)

        @pl.loop(0, groups)
        def _(group):
            waves = []
            for block in range(0, pairs, GROUP):
                column = jnp.zeros((GROUP, LANES), jnp.int32)
                for g in range(GROUP):
                    wave = wave_ref[(group ^ mask) * stride + first + 2 * (block + g)]
                    column = jnp.where(sublane == g, wave, column)
                waves.append(column)
            column = jnp.concatenate(waves, axis=0)
            column = jnp.where((column & 1) == odd_part, column, top - column)
            wide = column.astype(jnp.float32)
            weight = jnp.where(column == 0, 1.0, 2.0)
            cosine, sine = cos_sin(wide * lane)
            turn_cos, turn_sin = cos_sin(wide * float(LANES))
            cosine = cosine * weight
            sine = sine * -weight
            here = pl.ds(pl.multiple_of(begin + group * pairs, GROUP), pairs)
            for tile in range(FOLD // LANES + 1):
                if tile > 0:
                    cosine, sine = (
                        cosine * turn_cos + sine * turn_sin,
                        sine * turn_cos - cosine * turn_sin,
                    )
                block, at = divmod(tile * LANES, WIDTH)
                out_ref[block, 0, 0, here, pl.ds(at, LANES)] = cosine.astype(jnp.bfloat16)
                out_ref[block, 0, 1, here, pl.ds(at, LANES)] = sine.astype(jnp.bfloat16)

        begin += groups * pairs


def phase_table(wave_order, slots, counts):
    waves = wave_order.shape[0]
    pairs = waves // 2
    if len(counts) == 1:
        segments = ((waves // 64, 64, 0, 32, False),)
    else:
        segments = tuple(
            (waves // slots, slots, sum(counts[:n]), count // 2, n < len(counts) - 1)
            for n, count in enumerate(counts)
        )
    blocks = FOLD // WIDTH + 1
    return pl.pallas_call(
        functools.partial(table_kernel, segments=segments),
        out_shape=jax.ShapeDtypeStruct((blocks, 2, 2, pairs, WIDTH), jnp.bfloat16),
        grid_spec=pltpu.PrefetchScalarGridSpec(
            num_scalar_prefetch=1,
            grid=(2,),
            in_specs=[],
            out_specs=pl.BlockSpec(
                (blocks, 1, 2, pairs, WIDTH), lambda p, *_: (0, p, 0, 0, 0)
            ),
        ),
        compiler_params=pltpu.CompilerParams(vmem_limit_bytes=VMEM_LIMIT),
        cost_estimate=pl.CostEstimate(
            flops=16 * waves * FOLD, bytes_accessed=4 * waves * FOLD, transcendentals=0
        ),
        name="phases",
    )(wave_order)


def repack_kernel(*refs, shards):
    for turn, out in enumerate(refs[shards:]):
        for shift in range(shards):
            out[shift] = refs[shift][turn]


def repack(parts):
    shards = len(parts)
    groups, count, _ = parts[0].shape
    return pl.pallas_call(
        functools.partial(repack_kernel, shards=shards),
        out_shape=[jax.ShapeDtypeStruct((shards, count, LANES), jnp.bfloat16)] * groups,
        compiler_params=pltpu.CompilerParams(vmem_limit_bytes=VMEM_LIMIT),
        cost_estimate=pl.CostEstimate(
            flops=0, bytes_accessed=4 * groups * shards * count * LANES, transcendentals=0
        ),
        name="repack",
    )(*parts)


def arrange(block_of, shard_of, left, total, levels, begin):
    shards = left.shape[2] * 2 // LANES
    unit = one_hot(
        lax.broadcasted_iota(jnp.int32, (LANES, LANES), 0)
        == lax.broadcasted_iota(jnp.int32, (LANES, LANES), 1)
    )
    for odd in range(2):
        for shard in range(shards):
            turned = nt_dot(unit, block_of(shard, odd)).astype(jnp.bfloat16)
            for r in range(LANES // (2 * levels)):
                row = (r * shards + shard_of(shard)) * levels
                row = row if isinstance(row, int) else pl.multiple_of(row, levels)
                here = pl.ds(row, levels)
                for part in range(2):
                    at = (2 * r + part) * levels
                    left[odd, part, here, pl.ds(begin, total)] = turned[at : at + levels, :]


def fourier_kernel(*refs, levels, early):
    early_refs = refs[:early]
    got_ref, table_ref, out_ref = refs[early : early + 3]
    got, sooner, table, edge, left, back, result, fetched, arrived, done = refs[early + 3 :]
    blocks = table_ref.shape[0] - 1
    moves = [pltpu.make_async_copy(got_ref, got, fetched.at[0])]
    edge_move = pltpu.make_async_copy(
        table_ref.at[blocks, :, :, :, pl.ds(0, LANES)], edge, fetched.at[1]
    )
    for n, early_ref in enumerate(early_refs):
        moves.append(pltpu.make_async_copy(early_ref, sooner.at[n], fetched.at[n + 2]))
    order = list(range(blocks - 1, -1, -1))
    tables = {
        at: pltpu.make_async_copy(table_ref.at[at], table.at[at], arrived.at[at]) for at in order
    }
    for move in moves:
        move.start()
    for at in order:
        tables[at].start()
    edge_move.start()
    for move in moves:
        move.wait()
    groups, _, _, pairs, _ = got.shape
    begin = len(early_refs) * sooner.shape[3]

    def sooner_block(shift, odd):
        return sooner[:, shift, odd].reshape(begin, LANES)

    def got_block(shard, odd):
        return got[:, shard, odd].reshape(groups * pairs, LANES)

    if early:
        arrange(sooner_block, lambda shift: lax.axis_index("lev") ^ shift, left, begin, levels, 0)
    arrange(got_block, lambda shard: shard, left, groups * pairs, levels, begin)

    def combine(block):
        sums = [
            [
                jnp.dot(left[odd, part], block[odd, part], preferred_element_type=jnp.float32)
                for part in range(2)
            ]
            for odd in range(2)
        ]
        return [
            (sums[0][part] + sums[1][part], sums[0][part] - sums[1][part]) for part in range(2)
        ]

    mirror = one_hot(
        lax.broadcasted_iota(jnp.int32, (2 * LANES, LANES), 0)
        == LANES - lax.broadcasted_iota(jnp.int32, (2 * LANES, LANES), 1)
    )
    stores = []

    def reverse(first, tile):
        for side in range(2):
            turned = jnp.dot(
                back[side, :, pl.ds(first + tile * LANES, 2 * LANES)],
                mirror,
                preferred_element_type=jnp.float32,
            )
            to = (2 * side + 2) * FOLD - first - (tile + 1) * LANES
            result[:, pl.ds(to, LANES)] = turned.astype(jnp.bfloat16)

    def store(at, n, start):
        span = pl.ds(start, WIDTH)
        copy = pltpu.make_async_copy(result.at[:, span], out_ref.at[:, span], done.at[at, n])
        copy.start()
        stores.append(copy)

    tiles = WIDTH // LANES
    for at in order:
        tables[at].wait()
        (a, c), (b, d) = combine(table.at[at])
        first = at * WIDTH
        result[:, pl.ds(first, WIDTH)] = (a + b).astype(jnp.bfloat16)
        result[:, pl.ds(2 * FOLD + first, WIDTH)] = (c + d).astype(jnp.bfloat16)
        back[0, :, pl.ds(first, WIDTH)] = (c - d).astype(jnp.bfloat16)
        back[1, :, pl.ds(first, WIDTH)] = (a - b).astype(jnp.bfloat16)
        store(at, 0, first)
        store(at, 1, 2 * FOLD + first)
        outermost = at == blocks - 1
        for tile in range(tiles - 1 if outermost else tiles):
            reverse(first, tile)
        if not outermost:
            store(at, 2, 2 * FOLD - first - WIDTH)
            store(at, 3, 4 * FOLD - first - WIDTH)
    edge_move.wait()
    (a, c), (b, d) = combine(edge)
    back[0, :, pl.ds(FOLD, LANES)] = (c - d).astype(jnp.bfloat16)
    back[1, :, pl.ds(FOLD, LANES)] = (a - b).astype(jnp.bfloat16)
    reverse(FOLD - WIDTH, tiles - 1)
    store(blocks - 1, 2, FOLD)
    store(blocks - 1, 3, 3 * FOLD)
    for copy in stores:
        copy.wait()


def fourier_sum(early, got, table, levels):
    shards = got.shape[1]
    rows = shards * LANES // 2
    blocks, _, _, pairs, _ = table.shape
    blocks -= 1
    anywhere = pl.BlockSpec(memory_space=pl.ANY)
    return pl.pallas_call(
        functools.partial(fourier_kernel, levels=levels, early=len(early)),
        out_shape=jax.ShapeDtypeStruct((rows, NLON), jnp.bfloat16),
        in_specs=[anywhere] * (len(early) + 2),
        out_specs=anywhere,
        scratch_shapes=[
            pltpu.VMEM(got.shape, jnp.bfloat16),
            pltpu.VMEM((len(early), *early[0].shape) if early else got.shape, jnp.bfloat16),
            pltpu.VMEM((blocks, *table.shape[1:]), jnp.bfloat16),
            pltpu.VMEM((2, 2, pairs, LANES), jnp.bfloat16),
            pltpu.VMEM((2, 2, rows, pairs), jnp.bfloat16),
            pltpu.VMEM((2, rows, FOLD + LANES), jnp.bfloat16),
            pltpu.VMEM((rows, NLON), jnp.bfloat16),
            pltpu.SemaphoreType.DMA((len(early) + 2,)),
            pltpu.SemaphoreType.DMA((blocks,)),
            pltpu.SemaphoreType.DMA((blocks, 4)),
        ],
        compiler_params=pltpu.CompilerParams(vmem_limit_bytes=52 * 1024 * 1024),
        cost_estimate=pl.CostEstimate(
            flops=8 * rows * pairs * FOLD,
            bytes_accessed=8 * pairs * FOLD + 2 * rows * NLON,
            transcendentals=0,
        ),
        name="fourier",
    )(*early, got, table)


def swap(block, axis, offset):
    if offset == 0:
        return block
    size = lax.axis_size(axis)
    return lax.ppermute(block, axis, [(i, i ^ offset) for i in range(size)])


def chunk_counts(slots):
    if slots % (4 * GROUP):
        return (slots,)
    first = slots // 2 // (2 * GROUP) * (2 * GROUP)
    return (first, slots - first)


def local(spectra, polynomials, wave_order, row_cutoff):
    parts, levels, slots, degrees = spectra.shape
    groups = lax.axis_size("wave")
    shards = lax.axis_size("lev")
    basis = jnp.swapaxes(polynomials, 1, 2)
    counts = chunk_counts(slots)
    early = []
    offset = 0
    sent = []
    crossed = []
    for chunk, count in enumerate(counts):
        last = chunk == len(counts) - 1
        cutoff, *_ = lax.optimization_barrier((row_cutoff, *sent[:1]))
        sent = legendre(
            spectra, basis, wave_order, cutoff, offset, count, groups, shards, not last
        )
        offset += count
        if last:
            block = sent[0]
            if crossed:
                block, crossed = lax.optimization_barrier((sent[0], crossed))
                ready = repack(crossed)
                here = [swap(one, "wave", turn) for turn, one in enumerate(ready)]
                here = [one.reshape(shards, 2, counts[0] // 2, LANES) for one in here]
                early = here
            got = lax.all_to_all(block, ("wave", "lev"), 0, 0, tiled=True)
            got = got.reshape(groups, shards, 2, count // 2, LANES)
        else:
            crossed = [swap(block, "lev", shift) for shift, block in enumerate(sent)]
    table = phase_table(wave_order, slots, counts)
    grid = fourier_sum(early, got, table, levels)
    return grid.reshape(LANES // (parts * levels), shards * levels, NLON)


def solution(mesh):
    in_specs = (P(None, "lev", "wave", None), P("wave", None, None), P(), P())
    out_specs = P(("wave", "lev"), None, None)
    return jax.shard_map(local, mesh=mesh, in_specs=in_specs, out_specs=out_specs, check_vma=False)
```
